32 devices in a mesh: grp: 2 (over y), date: 4 (over z), row: 4 (over x, core).
Axes of the slice: x: 2, y: 2, z: 4, core: 2. Of those that a mesh axis runs over, the one named last changes fastest.
Arguments:
- stack_data: float32 [16, 2, 64, 512], P(('grp', 'date'), None, 'row'), parts along dimension 0, may hold values from -40 to 40, as said below
- plan: int32 [8], replicated, may hold values from 0 to 7, each once
Outputs:
- coherence: float32 [16, 8, 2, 64, 512], P(('grp', 'date'), None, None, 'row'), parts along dimension 0
The draws below stay inside these ranges and needn't reach their ends.
There are 2 independent parts, one for each index of `grp`. The reference program is written for one: setup_inputs(seed, part) draws one part's arguments, and reference() takes and returns one part's arrays. A program takes and returns all parts, laid end to end along the dimension named above; an argument that names none is the same for every part. Nothing has to cross between parts.
Inputs may be any that keep to these rules, and one draw needn't show every extreme that they name: `stack_data`: complex samples of one scene seen on every date, each date with its own phase, strength and noise.
All inputs are finite; a program needn't handle non-finite values.
Results may differ from the reference program's by a relative error of at most 0.00005.
Values sent between devices are 32-bit elements; how exact they have to be, the bound alone decides.
A program may use at most 64 MiB of HBM per device.

```python
import jax
import jax.numpy as jnp
from jax import lax

COLS = 512
HALF_ROWS = 4
HALF_COLS = 16
DATES = 8
ROWS = 64


def draw_stack_data(key, part):
    keys = jax.random.split(jax.random.fold_in(key, 17), 5)
    scene = jax.random.normal(keys[0], (2, ROWS, COLS), jnp.float32)
    phase = jax.random.uniform(keys[1], (DATES, 1, 1), jnp.float32, -3.14159, 3.14159)
    strength = jax.random.uniform(keys[2], (DATES, 1, 1), jnp.float32, 0.3, 1.5)
    noise_level = jnp.exp(jax.random.uniform(keys[3], (DATES, 1, 1, 1), jnp.float32, jnp.log(0.3), jnp.log(2.0)))
    noise = jax.random.normal(keys[4], (DATES, 2, ROWS, COLS), jnp.float32)
    turned_real = jnp.cos(phase) * scene[0][None] - jnp.sin(phase) * scene[1][None]
    turned_imag = jnp.sin(phase) * scene[0][None] + jnp.cos(phase) * scene[1][None]
    signal = strength[:, None] * jnp.stack([turned_real, turned_imag], axis=1)
    values = signal + noise_level * noise
    return jnp.clip(values, -40.0, 40.0)


def setup_inputs(seed: int = 0, part: int = 0) -> dict:
    arg_keys = jax.random.split(jax.random.key(seed), 3)
    part_keys = jax.random.split(jax.random.fold_in(arg_keys[2], part), 3)
    stack_data = draw_stack_data(jax.random.fold_in(jax.random.fold_in(arg_keys[2], part), 71), part)
    plan = jax.random.permutation(arg_keys[1], DATES).astype(jnp.int32)
    return {"stack_data": stack_data, "plan": plan}


def window_sum(field):
    lead = [(0, 0)] * (field.ndim - 2)
    padded = jnp.pad(field, lead + [(HALF_ROWS + 1, HALF_ROWS), (HALF_COLS + 1, HALF_COLS)])
    rowsum = jnp.cumsum(padded, axis=-2)
    rowsum = rowsum[..., 2 * HALF_ROWS + 1:, :] - rowsum[..., :ROWS, :]
    colsum = jnp.cumsum(rowsum, axis=-1)
    return colsum[..., 2 * HALF_COLS + 1:] - colsum[..., :COLS]

def reference(stack_data, plan):
    real_part = stack_data[:, 0]
    imag_part = stack_data[:, 1]
    power = window_sum(real_part * real_part + imag_part * imag_part)
    order_real = real_part[plan]
    order_imag = imag_part[plan]
    order_power = power[plan]

    def one_date(which):
        base_real = real_part[which]
        base_imag = imag_part[which]
        cross_real = window_sum(base_real[None] * order_real + base_imag[None] * order_imag)
        cross_imag = window_sum(base_imag[None] * order_real - base_real[None] * order_imag)
        factor = 1.0 / jnp.sqrt(power[which][None] * order_power + 1e-06)
        return jnp.stack([cross_real * factor, cross_imag * factor], axis=1)
    return lax.map(one_date, jnp.arange(DATES, dtype=jnp.int32))
```

```python
import functools

import jax
import jax.numpy as jnp
from jax import lax
from jax.experimental import pallas as pl
from jax.experimental.pallas import tpu as pltpu
from jax.sharding import PartitionSpec as P

HALF_ROWS = 4
HALF_COLS = 16
RIM = 8
LANES = 128

epsilon = 1e-06


def gather_kernel(n, rows_n, x_ref, coh, own, top, bot, band, pbuf, sbuf, lhs, pw,
                  load_sem, unit_recv, right_send, left_send, top_recv, bot_recv, down_send, up_send):
    local, _, height, width = x_ref.shape
    tiles = width // LANES
    me = lax.axis_index("date")
    row = lax.axis_index("row")
    right, left = lax.rem(me + 1, n), lax.rem(me + n - 1, n)
    has_up, has_down = row > 0, row < rows_n - 1
    even = n % 2 == 0
    full = (n - 1) // 2
    half = local // 2

    load = pltpu.make_async_copy(x_ref, own.at[me], load_sem)
    load.start()
    barrier = pltpu.get_barrier_semaphore()

    def greet(axis, index):
        pl.semaphore_signal(barrier, inc=1, device_id={axis: index}, device_id_type=pl.DeviceIdType.MESH)

    if n > 1:
        greet("date", right)
        greet("date", left)
    pl.when(has_up)(lambda: greet("row", row - 1))
    pl.when(has_down)(lambda: greet("row", row + 1))

    col_in = lax.broadcasted_iota(jnp.int32, (width, width), 0)
    col_out = lax.broadcasted_iota(jnp.int32, (width, width), 1)
    band[...] = jnp.where(jnp.abs(col_in - col_out) <= HALF_COLS, 1.0, 0.0).astype(jnp.bfloat16)

    @pl.when(row == 0)
    def _():
        top[...] = jnp.zeros_like(top)

    @pl.when(row == rows_n - 1)
    def _():
        bot[...] = jnp.zeros_like(bot)

    def remote(src, dst, send_sem, recv_sem, axis, index):
        return pltpu.make_async_remote_copy(
            src_ref=src, dst_ref=dst, send_sem=send_sem, recv_sem=recv_sem,
            device_id={axis: index}, device_id_type=pl.DeviceIdType.MESH)

    def to_right(s, l):
        return remote(own.at[s, l], own.at[s, l], right_send.at[s, l], unit_recv.at[s, l], "date", right)

    def to_left(s, l):
        return remote(own.at[s, l], own.at[s, l], left_send.at[s, l], unit_recv.at[s, l], "date", left)

    def to_down(s, l):
        return remote(own.at[s, l, :, pl.ds(height - RIM, RIM)], top.at[s, l], down_send.at[s, l],
                      top_recv.at[s, l], "row", row + 1)

    def to_up(s, l):
        return remote(own.at[s, l, :, pl.ds(0, RIM)], bot.at[s, l], up_send.at[s, l],
                      bot_recv.at[s, l], "row", row - 1)

    def send_rims(s, l):
        pl.when(has_down)(lambda: to_down(s, l).start())
        pl.when(has_up)(lambda: to_up(s, l).start())

    def wait_rims(s, l):
        pl.when(has_up)(lambda: to_down(s, l).wait_recv())
        pl.when(has_down)(lambda: to_up(s, l).wait_recv())

    def wait_rims_sent(s, l):
        pl.when(has_down)(lambda: to_down(s, l).wait_send())
        pl.when(has_up)(lambda: to_up(s, l).wait_send())

    def sample(s, l, part):
        return jnp.concatenate([top[s, l, part], own[s, l, part], bot[s, l, part]], axis=0)

    def window(fields):
        count = len(fields)
        for f, field in enumerate(fields):
            for c in range(tiles):
                pbuf[f, c] = field[:, c * LANES:(c + 1) * LANES]
        for f in range(count):
            sbuf[f] = (pbuf[f, :, 3:height + 11] + pbuf[f, :, 4:height + 12]) + pbuf[f, :, 5:height + 13]
        for f in range(count):
            total = (sbuf[f, :, 1:height + 1] + sbuf[f, :, 4:height + 4]) + sbuf[f, :, 7:height + 7]
            high = total.astype(jnp.bfloat16)
            low = (total - high.astype(jnp.float32)).astype(jnp.bfloat16)
            for c in range(tiles):
                lhs[f * height:(f + 1) * height, c * LANES:(c + 1) * LANES] = high[c]
                lhs[(count + f) * height:(count + f + 1) * height, c * LANES:(c + 1) * LANES] = low[c]
        sums = jnp.dot(lhs[0:2 * count * height], band[...], preferred_element_type=jnp.float32)
        return [sums[f * height:(f + 1) * height] + sums[(count + f) * height:(count + f + 1) * height]
                for f in range(count)]

    def local_power():
        fields = []
        for i in range(local):
            real, imag = sample(me, i, 0), sample(me, i, 1)
            fields.append(real * real + imag * imag)
        for i, power in enumerate(window(fields)):
            pw[i] = power

    def compute(s, l):
        oth_real, oth_imag = sample(s, l, 0), sample(s, l, 1)
        fields = [oth_real * oth_real + oth_imag * oth_imag]
        for i in range(local):
            real, imag = sample(me, i, 0), sample(me, i, 1)
            fields.append(real * oth_real + imag * oth_imag)
            fields.append(imag * oth_real - real * oth_imag)
        sums = window(fields)
        date = s * local + l
        for i in range(local):
            factor = lax.rsqrt(pw[i] * sums[0] + epsilon)
            coh[i, date, 0] = sums[1 + 2 * i] * factor
            coh[i, date, 1] = sums[2 + 2 * i] * factor

    load.wait()
    greeters = (2 if n > 1 else 0) + jnp.where(has_up, 1, 0) + jnp.where(has_down, 1, 0)
    pl.semaphore_wait(barrier, greeters)

    order = [(p, local - 1 - p) for p in range(local)]
    for p, q in order:
        if full >= 1 or (even and p < half):
            to_right(me, p).start()
        if full >= 1 or (even and q >= half):
            to_left(me, q).start()
    for l in range(local):
        send_rims(me, l)
    for l in range(local):
        wait_rims(me, l)
    local_power()
    for l in range(local):
        compute(me, l)

    def sources(t):
        return lax.rem(me + (n - 1) - t, n), lax.rem(me + 1 + t, n)

    def forwards(t, p, q, s_left, s_right, act_right, act_left):
        if even and p < half:
            act_right(s_left, p)
        else:
            pl.when(t < full - 1)(lambda: act_right(s_left, p))
        if even and q >= half:
            act_left(s_right, q)
        else:
            pl.when(t < full - 1)(lambda: act_left(s_right, q))

    def step(t, carry):
        s_left, s_right = sources(t)
        for p, q in order:
            to_right(s_left, p).wait_recv()
            to_left(s_right, q).wait_recv()
            forwards(t, p, q, s_left, s_right, lambda s, l: to_right(s, l).start(),
                     lambda s, l: to_left(s, l).start())
            send_rims(s_left, p)
            send_rims(s_right, q)
        for p, q in order:
            for s, l in ((s_left, p), (s_right, q)):
                wait_rims(s, l)
                compute(s, l)
        return carry

    if full >= 1:
        lax.fori_loop(0, full, step, 0)
    if even:
        far = lax.rem(me + n // 2, n)
        for l in range(local):
            (to_right if l < half else to_left)(far, l).wait_recv()
            send_rims(far, l)
        for l in range(local):
            wait_rims(far, l)
            compute(far, l)

    for p, q in order:
        if full >= 1 or (even and p < half):
            to_right(me, p).wait_send()
        if full >= 1 or (even and q >= half):
            to_left(me, q).wait_send()
    for l in range(local):
        wait_rims_sent(me, l)

    def drain(t, carry):
        s_left, s_right = sources(t)
        for p, q in order:
            forwards(t, p, q, s_left, s_right, lambda s, l: to_right(s, l).wait_send(),
                     lambda s, l: to_left(s, l).wait_send())
            wait_rims_sent(s_left, p)
            wait_rims_sent(s_right, q)
        return carry

    if full >= 1:
        lax.fori_loop(0, full, drain, 0)
    if even:
        for l in range(local):
            wait_rims_sent(far, l)


def order_kernel(plan_ref, coh, out, sem):
    dates = out.shape[1]

    def copy(k):
        return pltpu.make_async_copy(coh.at[:, plan_ref[k]], out.at[:, k], sem.at[k])

    def start(k, carry):
        copy(k).start()
        return carry

    def finish(k, carry):
        copy(k).wait()
        return carry

    lax.fori_loop(0, dates, start, 0)
    lax.fori_loop(0, dates, finish, 0)


def body(n, rows_n, stack_data, plan):
    local, _, height, width = stack_data.shape
    dates = local * n
    tiles = width // LANES
    fields = 2 * local + 1
    kind = jax.ShapeDtypeStruct((local, dates, 2, height, width), jnp.float32)
    dma = pltpu.SemaphoreType.DMA
    result_bytes = local * dates * 2 * height * width * 4
    coh = pl.pallas_call(
        functools.partial(gather_kernel, n, rows_n),
        out_shape=kind,
        in_specs=[pl.BlockSpec(memory_space=pl.ANY)],
        out_specs=pl.BlockSpec(memory_space=pltpu.VMEM),
        scratch_shapes=[
            pltpu.VMEM((n, local, 2, height, width), jnp.float32),
            pltpu.VMEM((n, local, 2, RIM, width), jnp.float32),
            pltpu.VMEM((n, local, 2, RIM, width), jnp.float32),
            pltpu.VMEM((width, width), jnp.bfloat16),
            pltpu.VMEM((fields, tiles, height + 2 * RIM, LANES), jnp.float32),
            pltpu.VMEM((fields, tiles, height + RIM, LANES), jnp.float32),
            pltpu.VMEM((2 * fields * height, width), jnp.bfloat16),
            pltpu.VMEM((local, height, width), jnp.float32),
            dma,
            dma((n, local)), dma((n, local)), dma((n, local)),
            dma((n, local)), dma((n, local)), dma((n, local)), dma((n, local)),
        ],
        compiler_params=pltpu.CompilerParams(
            collective_id=0, has_side_effects=True,
            vmem_limit_bytes=4 * result_bytes + (8 << 20)),
    )(stack_data)
    return pl.pallas_call(
        order_kernel,
        out_shape=kind,
        in_specs=[pl.BlockSpec(memory_space=pltpu.SMEM), pl.BlockSpec(memory_space=pltpu.VMEM)],
        out_specs=pl.BlockSpec(memory_space=pl.ANY),
        scratch_shapes=[dma((dates,))],
        compiler_params=pltpu.CompilerParams(vmem_limit_bytes=2 * result_bytes + (2 << 20)),
    )(plan, coh)


def solution(mesh):
    placed = (P(("grp", "date"), None, "row", None), P())
    return jax.shard_map(
        functools.partial(body, mesh.shape["date"], mesh.shape["row"]),
        mesh=mesh,
        in_specs=placed,
        out_specs=P(("grp", "date"), None, None, "row", None),
        check_vma=False,
    )
```

```python
import functools

import jax
import jax.numpy as jnp
from jax import lax
from jax.experimental import pallas as pl
from jax.experimental.pallas import tpu as pltpu
from jax.sharding import PartitionSpec as P

HALF_ROWS = 4
HALF_COLS = 16
RIM = 8
LANES = 128
VMEM_BYTES = 67043328

epsilon = 1e-06


def gather_kernel(n, rows_n, x_ref, coh, own, top, bot, band, pbuf, sbuf, lhs, pw,
                  load_sem, unit_recv, right_send, left_send, top_recv, bot_recv, down_send, up_send):
    local, _, height, width = x_ref.shape
    tiles = width // LANES
    me = lax.axis_index("date")
    row = lax.axis_index("row")
    has_left, has_right = me > 0, me < n - 1
    has_up, has_down = row > 0, row < rows_n - 1

    load = pltpu.make_async_copy(x_ref, own.at[me], load_sem)
    load.start()
    barrier = pltpu.get_barrier_semaphore()

    def greet(axis, index):
        pl.semaphore_signal(barrier, inc=1, device_id={axis: index}, device_id_type=pl.DeviceIdType.MESH)

    pl.when(has_left)(lambda: greet("date", me - 1))
    pl.when(has_right)(lambda: greet("date", me + 1))
    pl.when(has_up)(lambda: greet("row", row - 1))
    pl.when(has_down)(lambda: greet("row", row + 1))

    col_in = lax.broadcasted_iota(jnp.int32, (width, width), 0)
    col_out = lax.broadcasted_iota(jnp.int32, (width, width), 1)
    band[...] = jnp.where(jnp.abs(col_in - col_out) <= HALF_COLS, 1.0, 0.0).astype(jnp.bfloat16)

    @pl.when(row == 0)
    def _():
        top[...] = jnp.zeros_like(top)

    @pl.when(row == rows_n - 1)
    def _():
        bot[...] = jnp.zeros_like(bot)

    def remote(src, dst, send_sem, recv_sem, axis, index):
        return pltpu.make_async_remote_copy(
            src_ref=src, dst_ref=dst, send_sem=send_sem, recv_sem=recv_sem,
            device_id={axis: index}, device_id_type=pl.DeviceIdType.MESH)

    def to_right(s, l):
        return remote(own.at[s, l], own.at[s, l], right_send.at[s, l], unit_recv.at[s, l], "date", me + 1)

    def to_left(s, l):
        return remote(own.at[s, l], own.at[s, l], left_send.at[s, l], unit_recv.at[s, l], "date", me - 1)

    def to_down(s, l):
        return remote(own.at[s, l, :, pl.ds(height - RIM, RIM)], top.at[s, l], down_send.at[s, l],
                      top_recv.at[s, l], "row", row + 1)

    def to_up(s, l):
        return remote(own.at[s, l, :, pl.ds(0, RIM)], bot.at[s, l], up_send.at[s, l],
                      bot_recv.at[s, l], "row", row - 1)

    def send_rims(s, l):
        pl.when(has_down)(lambda: to_down(s, l).start())
        pl.when(has_up)(lambda: to_up(s, l).start())

    def wait_rims(s, l):
        pl.when(has_up)(lambda: to_down(s, l).wait_recv())
        pl.when(has_down)(lambda: to_up(s, l).wait_recv())

    def wait_rims_sent(s, l):
        pl.when(has_down)(lambda: to_down(s, l).wait_send())
        pl.when(has_up)(lambda: to_up(s, l).wait_send())

    def sample(s, l, part):
        return jnp.concatenate([top[s, l, part], own[s, l, part], bot[s, l, part]], axis=0)

    def window(fields):
        count = len(fields)
        for f, field in enumerate(fields):
            for c in range(tiles):
                pbuf[f, c] = field[:, c * LANES:(c + 1) * LANES]
        for f in range(count):
            sbuf[f] = (pbuf[f, :, 3:height + 11] + pbuf[f, :, 4:height + 12]) + pbuf[f, :, 5:height + 13]
        for f in range(count):
            total = (sbuf[f, :, 1:height + 1] + sbuf[f, :, 4:height + 4]) + sbuf[f, :, 7:height + 7]
            high = total.astype(jnp.bfloat16)
            low = (total - high.astype(jnp.float32)).astype(jnp.bfloat16)
            for c in range(tiles):
                lhs[f * height:(f + 1) * height, c * LANES:(c + 1) * LANES] = high[c]
                lhs[(count + f) * height:(count + f + 1) * height, c * LANES:(c + 1) * LANES] = low[c]
        sums = jnp.dot(lhs[0:2 * count * height], band[...], preferred_element_type=jnp.float32)
        return [sums[f * height:(f + 1) * height] + sums[(count + f) * height:(count + f + 1) * height]
                for f in range(count)]

    def local_power():
        fields = []
        for i in range(local):
            real, imag = sample(me, i, 0), sample(me, i, 1)
            fields.append(real * real + imag * imag)
        for i, power in enumerate(window(fields)):
            pw[i] = power

    def compute(s, l):
        oth_real, oth_imag = sample(s, l, 0), sample(s, l, 1)
        fields = [oth_real * oth_real + oth_imag * oth_imag]
        for i in range(local):
            real, imag = sample(me, i, 0), sample(me, i, 1)
            fields.append(real * oth_real + imag * oth_imag)
            fields.append(imag * oth_real - real * oth_imag)
        sums = window(fields)
        date = s * local + l
        for i in range(local):
            factor = lax.rsqrt(pw[i] * sums[0] + epsilon)
            coh[i, date, 0] = sums[1 + 2 * i] * factor
            coh[i, date, 1] = sums[2 + 2 * i] * factor

    load.wait()
    greeters = functools.reduce(jnp.add, [jnp.where(near, 1, 0) for near in (has_left, has_right, has_up, has_down)])
    pl.semaphore_wait(barrier, greeters)

    for l in range(local):
        pl.when(has_right)(lambda l=l: to_right(me, l).start())
        pl.when(has_left)(lambda l=l: to_left(me, l).start())
        send_rims(me, l)
    for l in range(local):
        wait_rims(me, l)
    local_power()
    for l in range(local):
        compute(me, l)

    def finish(t, l):
        for s, there in ((me - 1 - t, me - 1 - t >= 0), (me + 1 + t, me + 1 + t < n)):
            @pl.when(there)
            def _(s=s):
                wait_rims(s, l)
                compute(s, l)

    def step(t, carry):
        s_left, s_right = me - 1 - t, me + 1 + t
        for l in range(local):
            @pl.when(s_left >= 0)
            def _():
                to_right(s_left, l).wait_recv()
                pl.when(has_right)(lambda: to_right(s_left, l).start())
                send_rims(s_left, l)

            @pl.when(s_right < n)
            def _():
                to_left(s_right, l).wait_recv()
                pl.when(has_left)(lambda: to_left(s_right, l).start())
                send_rims(s_right, l)

            if l > 0:
                finish(t, l - 1)
            else:
                pl.when(t > 0)(lambda: finish(t - 1, local - 1))
        return carry

    if n > 1:
        lax.fori_loop(0, n - 1, step, 0)
        finish(n - 2, local - 1)

    for l in range(local):
        pl.when(has_right)(lambda l=l: to_right(me, l).wait_send())
        pl.when(has_left)(lambda l=l: to_left(me, l).wait_send())
        wait_rims_sent(me, l)

    def drain(t, carry):
        s_left, s_right = me - 1 - t, me + 1 + t
        for l in range(local):
            @pl.when(s_left >= 0)
            def _():
                pl.when(has_right)(lambda: to_right(s_left, l).wait_send())
                wait_rims_sent(s_left, l)

            @pl.when(s_right < n)
            def _():
                pl.when(has_left)(lambda: to_left(s_right, l).wait_send())
                wait_rims_sent(s_right, l)
        return carry

    if n > 1:
        lax.fori_loop(0, n - 1, drain, 0)


def order_kernel(plan_ref, coh, out, sem):
    dates = out.shape[1]

    def copy(k):
        return pltpu.make_async_copy(coh.at[:, plan_ref[k]], out.at[:, k], sem.at[k])

    def start(k, carry):
        copy(k).start()
        return carry

    def finish(k, carry):
        copy(k).wait()
        return carry

    lax.fori_loop(0, dates, start, 0)
    lax.fori_loop(0, dates, finish, 0)


def body(n, rows_n, stack_data, plan):
    local, _, height, width = stack_data.shape
    dates = local * n
    tiles = width // LANES
    fields = 2 * local + 1
    kind = jax.ShapeDtypeStruct((local, dates, 2, height, width), jnp.float32)
    dma = pltpu.SemaphoreType.DMA
    result_bytes = local * dates * 2 * height * width * 4
    coh = pl.pallas_call(
        functools.partial(gather_kernel, n, rows_n),
        out_shape=kind,
        in_specs=[pl.BlockSpec(memory_space=pltpu.HBM)],
        out_specs=pl.BlockSpec(memory_space=pltpu.VMEM),
        scratch_shapes=[
            pltpu.VMEM((n, local, 2, height, width), jnp.float32),
            pltpu.VMEM((n, local, 2, RIM, width), jnp.float32),
            pltpu.VMEM((n, local, 2, RIM, width), jnp.float32),
            pltpu.VMEM((width, width), jnp.bfloat16),
            pltpu.VMEM((fields, tiles, height + 2 * RIM, LANES), jnp.float32),
            pltpu.VMEM((fields, tiles, height + RIM, LANES), jnp.float32),
            pltpu.VMEM((2 * fields * height, width), jnp.bfloat16),
            pltpu.VMEM((local, height, width), jnp.float32),
            dma,
            dma((n, local)), dma((n, local)), dma((n, local)),
            dma((n, local)), dma((n, local)), dma((n, local)), dma((n, local)),
        ],
        compiler_params=pltpu.CompilerParams(
            collective_id=0, has_side_effects=True,
            vmem_limit_bytes=VMEM_BYTES - result_bytes - 2 * stack_data.size),
    )(stack_data)
    return pl.pallas_call(
        order_kernel,
        out_shape=kind,
        in_specs=[pl.BlockSpec(memory_space=pltpu.SMEM), pl.BlockSpec(memory_space=pltpu.VMEM)],
        out_specs=pl.BlockSpec(memory_space=pl.ANY),
        scratch_shapes=[dma((dates,))],
        compiler_params=pltpu.CompilerParams(vmem_limit_bytes=2 * result_bytes + (2 << 20)),
    )(plan, coh)


def solution(mesh):
    placed = (P(("grp", "date"), None, "row", None), P())
    return jax.shard_map(
        functools.partial(body, mesh.shape["date"], mesh.shape["row"]),
        mesh=mesh,
        in_specs=placed,
        out_specs=P(("grp", "date"), None, None, "row", None),
        check_vma=False,
    )
```

```python
import functools

import jax
import jax.numpy as jnp
from jax import lax
from jax.experimental import pallas as pl
from jax.experimental.pallas import tpu as pltpu
from jax.sharding import PartitionSpec as P

HALF_ROWS = 4
HALF_COLS = 16
RIM = 8
LANES = 128

epsilon = 1e-06


def gather_kernel(n, rows_n, x_ref, coh, own, top, bot, band, pbuf, sbuf, lhs, pw,
                  load_sem, unit_recv, right_send, left_send, top_recv, bot_recv, down_send, up_send):
    local, _, height, width = x_ref.shape
    tiles = width // LANES
    me = lax.axis_index("date")
    row = lax.axis_index("row")
    has_left, has_right = me > 0, me < n - 1
    has_up, has_down = row > 0, row < rows_n - 1

    load = pltpu.make_async_copy(x_ref, own.at[me], load_sem)
    load.start()
    barrier = pltpu.get_barrier_semaphore()

    def greet(axis, index):
        pl.semaphore_signal(barrier, inc=1, device_id={axis: index}, device_id_type=pl.DeviceIdType.MESH)

    pl.when(has_left)(lambda: greet("date", me - 1))
    pl.when(has_right)(lambda: greet("date", me + 1))
    pl.when(has_up)(lambda: greet("row", row - 1))
    pl.when(has_down)(lambda: greet("row", row + 1))

    col_in = lax.broadcasted_iota(jnp.int32, (width, width), 0)
    col_out = lax.broadcasted_iota(jnp.int32, (width, width), 1)
    band[...] = jnp.where(jnp.abs(col_in - col_out) <= HALF_COLS, 1.0, 0.0).astype(jnp.bfloat16)

    @pl.when(row == 0)
    def _():
        top[...] = jnp.zeros_like(top)

    @pl.when(row == rows_n - 1)
    def _():
        bot[...] = jnp.zeros_like(bot)

    def remote(src, dst, send_sem, recv_sem, axis, index):
        return pltpu.make_async_remote_copy(
            src_ref=src, dst_ref=dst, send_sem=send_sem, recv_sem=recv_sem,
            device_id={axis: index}, device_id_type=pl.DeviceIdType.MESH)

    def to_right(s, l):
        return remote(own.at[s, l], own.at[s, l], right_send.at[s, l], unit_recv.at[s, l], "date", me + 1)

    def to_left(s, l):
        return remote(own.at[s, l], own.at[s, l], left_send.at[s, l], unit_recv.at[s, l], "date", me - 1)

    def to_down(s, l):
        return remote(own.at[s, l, :, pl.ds(height - RIM, RIM)], top.at[s, l], down_send.at[s, l],
                      top_recv.at[s, l], "row", row + 1)

    def to_up(s, l):
        return remote(own.at[s, l, :, pl.ds(0, RIM)], bot.at[s, l], up_send.at[s, l],
                      bot_recv.at[s, l], "row", row - 1)

    def send_rims(s, l):
        pl.when(has_down)(lambda: to_down(s, l).start())
        pl.when(has_up)(lambda: to_up(s, l).start())

    def wait_rims(s, l):
        pl.when(has_up)(lambda: to_down(s, l).wait_recv())
        pl.when(has_down)(lambda: to_up(s, l).wait_recv())

    def wait_rims_sent(s, l):
        pl.when(has_down)(lambda: to_down(s, l).wait_send())
        pl.when(has_up)(lambda: to_up(s, l).wait_send())

    def sample(s, l, part):
        return jnp.concatenate([top[s, l, part], own[s, l, part], bot[s, l, part]], axis=0)

    def window(fields):
        count = len(fields)
        for f, field in enumerate(fields):
            for c in range(tiles):
                pbuf[f, c] = field[:, c * LANES:(c + 1) * LANES]
        for f in range(count):
            sbuf[f] = (pbuf[f, :, 3:height + 11] + pbuf[f, :, 4:height + 12]) + pbuf[f, :, 5:height + 13]
        for f in range(count):
            total = (sbuf[f, :, 1:height + 1] + sbuf[f, :, 4:height + 4]) + sbuf[f, :, 7:height + 7]
            high = total.astype(jnp.bfloat16)
            low = (total - high.astype(jnp.float32)).astype(jnp.bfloat16)
            for c in range(tiles):
                lhs[f * height:(f + 1) * height, c * LANES:(c + 1) * LANES] = high[c]
                lhs[(count + f) * height:(count + f + 1) * height, c * LANES:(c + 1) * LANES] = low[c]
        sums = jnp.dot(lhs[0:2 * count * height], band[...], preferred_element_type=jnp.float32)
        return [sums[f * height:(f + 1) * height] + sums[(count + f) * height:(count + f + 1) * height]
                for f in range(count)]

    def local_power():
        fields = []
        for i in range(local):
            real, imag = sample(me, i, 0), sample(me, i, 1)
            fields.append(real * real + imag * imag)
        for i, power in enumerate(window(fields)):
            pw[i] = power

    def compute(s, l):
        oth_real, oth_imag = sample(s, l, 0), sample(s, l, 1)
        fields = [oth_real * oth_real + oth_imag * oth_imag]
        for i in range(local):
            real, imag = sample(me, i, 0), sample(me, i, 1)
            fields.append(real * oth_real + imag * oth_imag)
            fields.append(imag * oth_real - real * oth_imag)
        sums = window(fields)
        date = s * local + l
        for i in range(local):
            factor = lax.rsqrt(pw[i] * sums[0] + epsilon)
            coh[i, date, 0] = sums[1 + 2 * i] * factor
            coh[i, date, 1] = sums[2 + 2 * i] * factor

    load.wait()
    greeters = functools.reduce(jnp.add, [jnp.where(near, 1, 0) for near in (has_left, has_right, has_up, has_down)])
    pl.semaphore_wait(barrier, greeters)

    for l in range(local):
        pl.when(has_right)(lambda l=l: to_right(me, l).start())
        pl.when(has_left)(lambda l=l: to_left(me, l).start())
        send_rims(me, l)
    for l in range(local):
        wait_rims(me, l)
    local_power()
    for l in range(local):
        compute(me, l)

    def finish(t, l):
        for s, there in ((me - 1 - t, me - 1 - t >= 0), (me + 1 + t, me + 1 + t < n)):
            @pl.when(there)
            def _(s=s):
                wait_rims(s, l)
                compute(s, l)

    def step(t, carry):
        s_left, s_right = me - 1 - t, me + 1 + t
        for l in range(local):
            @pl.when(s_left >= 0)
            def _():
                to_right(s_left, l).wait_recv()
                pl.when(has_right)(lambda: to_right(s_left, l).start())
                send_rims(s_left, l)

            @pl.when(s_right < n)
            def _():
                to_left(s_right, l).wait_recv()
                pl.when(has_left)(lambda: to_left(s_right, l).start())
                send_rims(s_right, l)

            if l > 0:
                finish(t, l - 1)
            else:
                pl.when(t > 0)(lambda: finish(t - 1, local - 1))
        return carry

    if n > 1:
        lax.fori_loop(0, n - 1, step, 0)
        finish(n - 2, local - 1)

    for l in range(local):
        pl.when(has_right)(lambda l=l: to_right(me, l).wait_send())
        pl.when(has_left)(lambda l=l: to_left(me, l).wait_send())
        wait_rims_sent(me, l)

    def drain(t, carry):
        s_left, s_right = me - 1 - t, me + 1 + t
        for l in range(local):
            @pl.when(s_left >= 0)
            def _():
                pl.when(has_right)(lambda: to_right(s_left, l).wait_send())
                wait_rims_sent(s_left, l)

            @pl.when(s_right < n)
            def _():
                pl.when(has_left)(lambda: to_left(s_right, l).wait_send())
                wait_rims_sent(s_right, l)
        return carry

    if n > 1:
        lax.fori_loop(0, n - 1, drain, 0)


def order_kernel(plan_ref, coh, out, sem):
    dates = out.shape[1]

    def copy(k):
        return pltpu.make_async_copy(coh.at[:, plan_ref[k]], out.at[:, k], sem.at[k])

    def start(k, carry):
        copy(k).start()
        return carry

    def finish(k, carry):
        copy(k).wait()
        return carry

    lax.fori_loop(0, dates, start, 0)
    lax.fori_loop(0, dates, finish, 0)


def body(n, rows_n, stack_data, plan):
    local, _, height, width = stack_data.shape
    dates = local * n
    tiles = width // LANES
    fields = 2 * local + 1
    kind = jax.ShapeDtypeStruct((local, dates, 2, height, width), jnp.float32)
    dma = pltpu.SemaphoreType.DMA
    result_bytes = local * dates * 2 * height * width * 4
    stack_data = pltpu.with_memory_space_constraint(stack_data, pltpu.HBM)
    coh = pl.pallas_call(
        functools.partial(gather_kernel, n, rows_n),
        out_shape=kind,
        in_specs=[pl.BlockSpec(memory_space=pltpu.HBM)],
        out_specs=pl.BlockSpec(memory_space=pltpu.VMEM),
        scratch_shapes=[
            pltpu.VMEM((n, local, 2, height, width), jnp.float32),
            pltpu.VMEM((n, local, 2, RIM, width), jnp.float32),
            pltpu.VMEM((n, local, 2, RIM, width), jnp.float32),
            pltpu.VMEM((width, width), jnp.bfloat16),
            pltpu.VMEM((fields, tiles, height + 2 * RIM, LANES), jnp.float32),
            pltpu.VMEM((fields, tiles, height + RIM, LANES), jnp.float32),
            pltpu.VMEM((2 * fields * height, width), jnp.bfloat16),
            pltpu.VMEM((local, height, width), jnp.float32),
            dma,
            dma((n, local)), dma((n, local)), dma((n, local)),
            dma((n, local)), dma((n, local)), dma((n, local)), dma((n, local)),
        ],
        compiler_params=pltpu.CompilerParams(
            collective_id=0, has_side_effects=True,
            vmem_limit_bytes=4 * result_bytes + (8 << 20)),
    )(stack_data)
    return pl.pallas_call(
        order_kernel,
        out_shape=kind,
        in_specs=[pl.BlockSpec(memory_space=pltpu.SMEM), pl.BlockSpec(memory_space=pltpu.VMEM)],
        out_specs=pl.BlockSpec(memory_space=pl.ANY),
        scratch_shapes=[dma((dates,))],
        compiler_params=pltpu.CompilerParams(vmem_limit_bytes=2 * result_bytes + (2 << 20)),
    )(plan, coh)


def solution(mesh):
    placed = (P(("grp", "date"), None, "row", None), P())
    return jax.shard_map(
        functools.partial(body, mesh.shape["date"], mesh.shape["row"]),
        mesh=mesh,
        in_specs=placed,
        out_specs=P(("grp", "date"), None, None, "row", None),
        check_vma=False,
    )
```

```python
import functools

import jax
import jax.numpy as jnp
from jax import lax
from jax.experimental import pallas as pl
from jax.experimental.pallas import tpu as pltpu
from jax.sharding import PartitionSpec as P

HALF_ROWS = 4
HALF_COLS = 16
LANES = 128

epsilon = 1e-06


def gather_kernel(n, rows_n, x_ref, coh, own, edge, mid, top, bot, mine, other, band, pbuf, sbuf, lhs, pw,
                  load_sem, recv, right_send, left_send, top_recv, bot_recv, down_send, up_send):
    local, _, height, width = x_ref.shape
    tiles = width // LANES
    inner = height - 2 * HALF_ROWS
    span = height + 2 * HALF_ROWS
    me = lax.axis_index("date")
    row = lax.axis_index("row")
    has_left, has_right = me > 0, me < n - 1
    has_up, has_down = row > 0, row < rows_n - 1

    load = pltpu.make_async_copy(x_ref, own, load_sem)
    load.start()
    barrier = pltpu.get_barrier_semaphore()

    def greet(axis, index):
        pl.semaphore_signal(barrier, inc=1, device_id={axis: index}, device_id_type=pl.DeviceIdType.MESH)

    pl.when(has_left)(lambda: greet("date", me - 1))
    pl.when(has_right)(lambda: greet("date", me + 1))
    pl.when(has_up)(lambda: greet("row", row - 1))
    pl.when(has_down)(lambda: greet("row", row + 1))

    col_in = lax.broadcasted_iota(jnp.int32, (width, width), 0)
    col_out = lax.broadcasted_iota(jnp.int32, (width, width), 1)
    band[...] = jnp.where(jnp.abs(col_in - col_out) <= HALF_COLS, 1.0, 0.0).astype(jnp.bfloat16)

    @pl.when(row == 0)
    def _():
        top[...] = jnp.zeros_like(top)

    @pl.when(row == rows_n - 1)
    def _():
        bot[...] = jnp.zeros_like(bot)

    def remote(src, dst, send_sem, recv_sem, axis, index):
        return pltpu.make_async_remote_copy(
            src_ref=src, dst_ref=dst, send_sem=send_sem, recv_sem=recv_sem,
            device_id={axis: index}, device_id_type=pl.DeviceIdType.MESH)

    chunks = [(0, l) for l in range(local)] + [(1, l) for l in range(local)]

    def to_date(sends, step, k, s, l):
        ref = (edge, mid)[k].at[s, l]
        return remote(ref, ref, sends.at[k, s, l], recv.at[k, s, l], "date", me + step)

    def to_right(k, s, l):
        return to_date(right_send, 1, k, s, l)

    def to_left(k, s, l):
        return to_date(left_send, -1, k, s, l)

    def to_down(s, l):
        return remote(edge.at[s, l, 1], top.at[s, l], down_send.at[s, l], top_recv.at[s, l], "row", row + 1)

    def to_up(s, l):
        return remote(edge.at[s, l, 0], bot.at[s, l], up_send.at[s, l], bot_recv.at[s, l], "row", row - 1)

    def send_rims(s, l):
        pl.when(has_down)(lambda: to_down(s, l).start())
        pl.when(has_up)(lambda: to_up(s, l).start())

    def wait_rims(s, l):
        pl.when(has_up)(lambda: to_down(s, l).wait_recv())
        pl.when(has_down)(lambda: to_up(s, l).wait_recv())

    def wait_rims_sent(s, l):
        pl.when(has_down)(lambda: to_down(s, l).wait_send())
        pl.when(has_up)(lambda: to_up(s, l).wait_send())

    def assemble(dst, s, l):
        low = height + HALF_ROWS
        for part in range(2):
            for c in range(tiles):
                lanes = slice(c * LANES, (c + 1) * LANES)
                dst[part, c, 0:HALF_ROWS] = top[s, l, part, :, lanes]
                dst[part, c, HALF_ROWS:2 * HALF_ROWS] = edge[s, l, 0, part, :, lanes]
                dst[part, c, 2 * HALF_ROWS:2 * HALF_ROWS + inner] = mid[s, l, part, :, lanes]
                dst[part, c, height:low] = edge[s, l, 1, part, :, lanes]
                dst[part, c, low:low + HALF_ROWS] = bot[s, l, part, :, lanes]

    def window(fields):
        count = len(fields)
        for f, field in enumerate(fields):
            pbuf[f] = field
        for f in range(count):
            sbuf[f, :, 0:span - 2] = (pbuf[f, :, 0:span - 2] + pbuf[f, :, 1:span - 1]) + pbuf[f, :, 2:span]
        for f in range(count):
            total = (sbuf[f, :, 0:height] + sbuf[f, :, 3:height + 3]) + sbuf[f, :, 6:height + 6]
            high = total.astype(jnp.bfloat16)
            low = (total - high.astype(jnp.float32)).astype(jnp.bfloat16)
            for c in range(tiles):
                lhs[f * height:(f + 1) * height, c * LANES:(c + 1) * LANES] = high[c]
                lhs[(count + f) * height:(count + f + 1) * height, c * LANES:(c + 1) * LANES] = low[c]
        sums = jnp.dot(lhs[0:2 * count * height], band[...], preferred_element_type=jnp.float32)
        return [sums[f * height:(f + 1) * height] + sums[(count + f) * height:(count + f + 1) * height]
                for f in range(count)]

    def local_power():
        fields = []
        for i in range(local):
            real, imag = mine[i, 0], mine[i, 1]
            fields.append(real * real + imag * imag)
        for i, power in enumerate(window(fields)):
            pw[i] = power

    def compute(s, l, oth_real, oth_imag):
        fields = [oth_real * oth_real + oth_imag * oth_imag]
        for i in range(local):
            real, imag = mine[i, 0], mine[i, 1]
            fields.append(real * oth_real + imag * oth_imag)
            fields.append(imag * oth_real - real * oth_imag)
        sums = window(fields)
        date = s * local + l
        for i in range(local):
            factor = lax.rsqrt(pw[i] * sums[0] + epsilon)
            coh[i, date, 0] = sums[1 + 2 * i] * factor
            coh[i, date, 1] = sums[2 + 2 * i] * factor

    load.wait()
    for l in range(local):
        edge[me, l, 0] = own[l, :, 0:HALF_ROWS]
        edge[me, l, 1] = own[l, :, height - HALF_ROWS:height]
        mid[me, l] = own[l, :, HALF_ROWS:height - HALF_ROWS]
    greeters = functools.reduce(jnp.add, [jnp.where(near, 1, 0) for near in (has_left, has_right, has_up, has_down)])
    pl.semaphore_wait(barrier, greeters)

    for k, l in chunks:
        pl.when(has_right)(lambda: to_right(k, me, l).start())
        pl.when(has_left)(lambda: to_left(k, me, l).start())
        if k == 0:
            send_rims(me, l)
    for l in range(local):
        wait_rims(me, l)
        assemble(mine.at[l], me, l)
    local_power()
    for l in range(local):
        compute(me, l, mine[l, 0], mine[l, 1])

    def finish(t, l):
        for s, there in ((me - 1 - t, me - 1 - t >= 0), (me + 1 + t, me + 1 + t < n)):
            @pl.when(there)
            def _(s=s):
                wait_rims(s, l)
                assemble(other, s, l)
                compute(s, l, other[0], other[1])

    def step(t, carry):
        s_left, s_right = me - 1 - t, me + 1 + t
        for k, l in chunks:
            @pl.when(s_left >= 0)
            def _():
                to_right(k, s_left, l).wait_recv()
                pl.when(has_right)(lambda: to_right(k, s_left, l).start())
                if k == 0:
                    send_rims(s_left, l)

            @pl.when(s_right < n)
            def _():
                to_left(k, s_right, l).wait_recv()
                pl.when(has_left)(lambda: to_left(k, s_right, l).start())
                if k == 0:
                    send_rims(s_right, l)

            if k == 1 and l > 0:
                finish(t, l - 1)
            if k == 0 and l == 0:
                pl.when(t > 0)(lambda: finish(t - 1, local - 1))
        return carry

    if n > 1:
        lax.fori_loop(0, n - 1, step, 0)
        finish(n - 2, local - 1)

    for k, l in chunks:
        pl.when(has_right)(lambda: to_right(k, me, l).wait_send())
        pl.when(has_left)(lambda: to_left(k, me, l).wait_send())
        if k == 0:
            wait_rims_sent(me, l)

    def drain(t, carry):
        s_left, s_right = me - 1 - t, me + 1 + t
        for k, l in chunks:
            @pl.when(s_left >= 0)
            def _():
                pl.when(has_right)(lambda: to_right(k, s_left, l).wait_send())
                if k == 0:
                    wait_rims_sent(s_left, l)

            @pl.when(s_right < n)
            def _():
                pl.when(has_left)(lambda: to_left(k, s_right, l).wait_send())
                if k == 0:
                    wait_rims_sent(s_right, l)
        return carry

    if n > 1:
        lax.fori_loop(0, n - 1, drain, 0)


def order_kernel(plan_ref, coh, out, sem):
    dates = out.shape[1]

    def copy(k):
        return pltpu.make_async_copy(coh.at[:, plan_ref[k]], out.at[:, k], sem.at[k])

    def start(k, carry):
        copy(k).start()
        return carry

    def finish(k, carry):
        copy(k).wait()
        return carry

    lax.fori_loop(0, dates, start, 0)
    lax.fori_loop(0, dates, finish, 0)


def body(n, rows_n, stack_data, plan):
    local, _, height, width = stack_data.shape
    dates = local * n
    tiles = width // LANES
    fields = 2 * local + 1
    span = height + 2 * HALF_ROWS
    kind = jax.ShapeDtypeStruct((local, dates, 2, height, width), jnp.float32)
    dma = pltpu.SemaphoreType.DMA
    result_bytes = local * dates * 2 * height * width * 4
    stack_data = pltpu.with_memory_space_constraint(stack_data, pltpu.HBM)
    coh = pl.pallas_call(
        functools.partial(gather_kernel, n, rows_n),
        out_shape=kind,
        in_specs=[pl.BlockSpec(memory_space=pltpu.HBM)],
        out_specs=pl.BlockSpec(memory_space=pltpu.VMEM),
        scratch_shapes=[
            pltpu.VMEM((local, 2, height, width), jnp.float32),
            pltpu.VMEM((n, local, 2, 2, HALF_ROWS, width), jnp.float32),
            pltpu.VMEM((n, local, 2, height - 2 * HALF_ROWS, width), jnp.float32),
            pltpu.VMEM((n, local, 2, HALF_ROWS, width), jnp.float32),
            pltpu.VMEM((n, local, 2, HALF_ROWS, width), jnp.float32),
            pltpu.VMEM((local, 2, tiles, span, LANES), jnp.float32),
            pltpu.VMEM((2, tiles, span, LANES), jnp.float32),
            pltpu.VMEM((width, width), jnp.bfloat16),
            pltpu.VMEM((fields, tiles, span, LANES), jnp.float32),
            pltpu.VMEM((fields, tiles, span, LANES), jnp.float32),
            pltpu.VMEM((2 * fields * height, width), jnp.bfloat16),
            pltpu.VMEM((local, height, width), jnp.float32),
            dma,
            dma((2, n, local)), dma((2, n, local)), dma((2, n, local)),
            dma((n, local)), dma((n, local)), dma((n, local)), dma((n, local)),
        ],
        compiler_params=pltpu.CompilerParams(
            collective_id=0, has_side_effects=True,
            vmem_limit_bytes=4 * result_bytes + (8 << 20)),
    )(stack_data)
    return pl.pallas_call(
        order_kernel,
        out_shape=kind,
        in_specs=[pl.BlockSpec(memory_space=pltpu.SMEM), pl.BlockSpec(memory_space=pltpu.VMEM)],
        out_specs=pl.BlockSpec(memory_space=pl.ANY),
        scratch_shapes=[dma((dates,))],
        compiler_params=pltpu.CompilerParams(vmem_limit_bytes=2 * result_bytes + (2 << 20)),
    )(plan, coh)


def solution(mesh):
    placed = (P(("grp", "date"), None, "row", None), P())
    return jax.shard_map(
        functools.partial(body, mesh.shape["date"], mesh.shape["row"]),
        mesh=mesh,
        in_specs=placed,
        out_specs=P(("grp", "date"), None, None, "row", None),
        check_vma=False,
    )
```

```python
import functools

import jax
import jax.numpy as jnp
from jax import lax
from jax.experimental import pallas as pl
from jax.experimental.pallas import tpu as pltpu
from jax.sharding import PartitionSpec as P

HALF_ROWS = 4
HALF_COLS = 16
LANES = 128

epsilon = 1e-06


def gather_kernel(n, rows_n, x_ref, coh, own, edge, mid, top, bot, mine, other, band, pbuf, sbuf, lhs, pw,
                  load_sem, recv, right_send, left_send, top_recv, bot_recv, down_send, up_send):
    local, _, height, width = x_ref.shape
    tiles = width // LANES
    inner = height - 2 * HALF_ROWS
    span = height + 2 * HALF_ROWS
    me = lax.axis_index("date")
    row = lax.axis_index("row")
    has_left, has_right = me > 0, me < n - 1
    has_up, has_down = row > 0, row < rows_n - 1

    load = pltpu.make_async_copy(x_ref, own, load_sem)
    load.start()
    barrier = pltpu.get_barrier_semaphore()

    def greet(axis, index):
        pl.semaphore_signal(barrier, inc=1, device_id={axis: index}, device_id_type=pl.DeviceIdType.MESH)

    pl.when(has_left)(lambda: greet("date", me - 1))
    pl.when(has_right)(lambda: greet("date", me + 1))
    pl.when(has_up)(lambda: greet("row", row - 1))
    pl.when(has_down)(lambda: greet("row", row + 1))

    col_in = lax.broadcasted_iota(jnp.int32, (width, width), 0)
    col_out = lax.broadcasted_iota(jnp.int32, (width, width), 1)
    band[...] = jnp.where(jnp.abs(col_in - col_out) <= HALF_COLS, 1.0, 0.0).astype(jnp.bfloat16)

    @pl.when(row == 0)
    def _():
        top[...] = jnp.zeros_like(top)

    @pl.when(row == rows_n - 1)
    def _():
        bot[...] = jnp.zeros_like(bot)

    def remote(src, dst, send_sem, recv_sem, axis, index):
        return pltpu.make_async_remote_copy(
            src_ref=src, dst_ref=dst, send_sem=send_sem, recv_sem=recv_sem,
            device_id={axis: index}, device_id_type=pl.DeviceIdType.MESH)

    chunks = [(0, l) for l in range(local)] + [(1, l) for l in range(local)]

    def to_date(sends, step, k, s, l):
        ref = (edge, mid)[k].at[s, l]
        return remote(ref, ref, sends.at[k, s, l], recv.at[k, s, l], "date", me + step)

    def to_right(k, s, l):
        return to_date(right_send, 1, k, s, l)

    def to_left(k, s, l):
        return to_date(left_send, -1, k, s, l)

    def to_down(s, l):
        return remote(edge.at[s, l, 1], top.at[s, l], down_send.at[s, l], top_recv.at[s, l], "row", row + 1)

    def to_up(s, l):
        return remote(edge.at[s, l, 0], bot.at[s, l], up_send.at[s, l], bot_recv.at[s, l], "row", row - 1)

    def send_rims(s, l):
        pl.when(has_down)(lambda: to_down(s, l).start())
        pl.when(has_up)(lambda: to_up(s, l).start())

    def wait_rims(s, l):
        pl.when(has_up)(lambda: to_down(s, l).wait_recv())
        pl.when(has_down)(lambda: to_up(s, l).wait_recv())

    def wait_rims_sent(s, l):
        pl.when(has_down)(lambda: to_down(s, l).wait_send())
        pl.when(has_up)(lambda: to_up(s, l).wait_send())

    def assemble(dst, s, l):
        low = height + HALF_ROWS
        for part in range(2):
            for c in range(tiles):
                lanes = slice(c * LANES, (c + 1) * LANES)
                dst[part, c, 0:HALF_ROWS] = top[s, l, part, :, lanes]
                dst[part, c, HALF_ROWS:2 * HALF_ROWS] = edge[s, l, 0, part, :, lanes]
                dst[part, c, 2 * HALF_ROWS:2 * HALF_ROWS + inner] = mid[s, l, part, :, lanes]
                dst[part, c, height:low] = edge[s, l, 1, part, :, lanes]
                dst[part, c, low:low + HALF_ROWS] = bot[s, l, part, :, lanes]

    def window(fields):
        count = len(fields)
        for f, field in enumerate(fields):
            pbuf[f] = field
        for f in range(count):
            sbuf[f, :, 0:span - 2] = (pbuf[f, :, 0:span - 2] + pbuf[f, :, 1:span - 1]) + pbuf[f, :, 2:span]
        for f in range(count):
            total = (sbuf[f, :, 0:height] + sbuf[f, :, 3:height + 3]) + sbuf[f, :, 6:height + 6]
            high = total.astype(jnp.bfloat16)
            low = (total - high.astype(jnp.float32)).astype(jnp.bfloat16)
            for c in range(tiles):
                lhs[f * height:(f + 1) * height, c * LANES:(c + 1) * LANES] = high[c]
                lhs[(count + f) * height:(count + f + 1) * height, c * LANES:(c + 1) * LANES] = low[c]
        sums = jnp.dot(lhs[0:2 * count * height], band[...], preferred_element_type=jnp.float32)
        return [sums[f * height:(f + 1) * height] + sums[(count + f) * height:(count + f + 1) * height]
                for f in range(count)]

    def local_power():
        fields = []
        for i in range(local):
            real, imag = mine[i, 0], mine[i, 1]
            fields.append(real * real + imag * imag)
        for i, power in enumerate(window(fields)):
            pw[i] = power

    def compute(s, l, oth_real, oth_imag):
        fields = [oth_real * oth_real + oth_imag * oth_imag]
        for i in range(local):
            real, imag = mine[i, 0], mine[i, 1]
            fields.append(real * oth_real + imag * oth_imag)
            fields.append(imag * oth_real - real * oth_imag)
        sums = window(fields)
        date = s * local + l
        for i in range(local):
            factor = lax.rsqrt(pw[i] * sums[0] + epsilon)
            coh[i, date, 0] = sums[1 + 2 * i] * factor
            coh[i, date, 1] = sums[2 + 2 * i] * factor

    load.wait()
    for l in range(local):
        edge[me, l, 0] = own[l, :, 0:HALF_ROWS]
        edge[me, l, 1] = own[l, :, height - HALF_ROWS:height]
        mid[me, l] = own[l, :, HALF_ROWS:height - HALF_ROWS]
    greeters = functools.reduce(jnp.add, [jnp.where(near, 1, 0) for near in (has_left, has_right, has_up, has_down)])
    pl.semaphore_wait(barrier, greeters)

    for k, l in chunks:
        pl.when(has_right)(lambda: to_right(k, me, l).start())
        pl.when(has_left)(lambda: to_left(k, me, l).start())
        if k == 0:
            send_rims(me, l)
    def own_dates():
        for l in range(local):
            wait_rims(me, l)
            assemble(mine.at[l], me, l)
        local_power()
        for l in range(local):
            compute(me, l, mine[l, 0], mine[l, 1])

    def finish(t, l):
        for s, there in ((me - 1 - t, me - 1 - t >= 0), (me + 1 + t, me + 1 + t < n)):
            @pl.when(there)
            def _(s=s):
                wait_rims(s, l)
                assemble(other, s, l)
                compute(s, l, other[0], other[1])

    def step(t, carry):
        s_left, s_right = me - 1 - t, me + 1 + t
        for k, l in chunks:
            @pl.when(s_left >= 0)
            def _():
                to_right(k, s_left, l).wait_recv()
                pl.when(has_right)(lambda: to_right(k, s_left, l).start())
                if k == 0:
                    send_rims(s_left, l)

            @pl.when(s_right < n)
            def _():
                to_left(k, s_right, l).wait_recv()
                pl.when(has_left)(lambda: to_left(k, s_right, l).start())
                if k == 0:
                    send_rims(s_right, l)

            if k == 0 and l == local - 1:
                pl.when(t == 0)(own_dates)
            if k == 1:
                finish(t, l)
        return carry

    if n > 1:
        lax.fori_loop(0, n - 1, step, 0)
    else:
        own_dates()

    for k, l in chunks:
        pl.when(has_right)(lambda: to_right(k, me, l).wait_send())
        pl.when(has_left)(lambda: to_left(k, me, l).wait_send())
        if k == 0:
            wait_rims_sent(me, l)

    def drain(t, carry):
        s_left, s_right = me - 1 - t, me + 1 + t
        for k, l in chunks:
            @pl.when(s_left >= 0)
            def _():
                pl.when(has_right)(lambda: to_right(k, s_left, l).wait_send())
                if k == 0:
                    wait_rims_sent(s_left, l)

            @pl.when(s_right < n)
            def _():
                pl.when(has_left)(lambda: to_left(k, s_right, l).wait_send())
                if k == 0:
                    wait_rims_sent(s_right, l)
        return carry

    if n > 1:
        lax.fori_loop(0, n - 1, drain, 0)


def order_kernel(plan_ref, coh, out, sem):
    dates = out.shape[1]

    def copy(k):
        return pltpu.make_async_copy(coh.at[:, plan_ref[k]], out.at[:, k], sem.at[k])

    def start(k, carry):
        copy(k).start()
        return carry

    def finish(k, carry):
        copy(k).wait()
        return carry

    lax.fori_loop(0, dates, start, 0)
    lax.fori_loop(0, dates, finish, 0)


def body(n, rows_n, stack_data, plan):
    local, _, height, width = stack_data.shape
    dates = local * n
    tiles = width // LANES
    fields = 2 * local + 1
    span = height + 2 * HALF_ROWS
    kind = jax.ShapeDtypeStruct((local, dates, 2, height, width), jnp.float32)
    dma = pltpu.SemaphoreType.DMA
    result_bytes = local * dates * 2 * height * width * 4
    stack_data = pltpu.with_memory_space_constraint(stack_data, pltpu.HBM)
    coh = pl.pallas_call(
        functools.partial(gather_kernel, n, rows_n),
        out_shape=kind,
        in_specs=[pl.BlockSpec(memory_space=pltpu.HBM)],
        out_specs=pl.BlockSpec(memory_space=pltpu.VMEM),
        scratch_shapes=[
            pltpu.VMEM((local, 2, height, width), jnp.float32),
            pltpu.VMEM((n, local, 2, 2, HALF_ROWS, width), jnp.float32),
            pltpu.VMEM((n, local, 2, height - 2 * HALF_ROWS, width), jnp.float32),
            pltpu.VMEM((n, local, 2, HALF_ROWS, width), jnp.float32),
            pltpu.VMEM((n, local, 2, HALF_ROWS, width), jnp.float32),
            pltpu.VMEM((local, 2, tiles, span, LANES), jnp.float32),
            pltpu.VMEM((2, tiles, span, LANES), jnp.float32),
            pltpu.VMEM((width, width), jnp.bfloat16),
            pltpu.VMEM((fields, tiles, span, LANES), jnp.float32),
            pltpu.VMEM((fields, tiles, span, LANES), jnp.float32),
            pltpu.VMEM((2 * fields * height, width), jnp.bfloat16),
            pltpu.VMEM((local, height, width), jnp.float32),
            dma,
            dma((2, n, local)), dma((2, n, local)), dma((2, n, local)),
            dma((n, local)), dma((n, local)), dma((n, local)), dma((n, local)),
        ],
        compiler_params=pltpu.CompilerParams(
            collective_id=0, has_side_effects=True,
            vmem_limit_bytes=4 * result_bytes + (8 << 20)),
    )(stack_data)
    return pl.pallas_call(
        order_kernel,
        out_shape=kind,
        in_specs=[pl.BlockSpec(memory_space=pltpu.SMEM), pl.BlockSpec(memory_space=pltpu.VMEM)],
        out_specs=pl.BlockSpec(memory_space=pl.ANY),
        scratch_shapes=[dma((dates,))],
        compiler_params=pltpu.CompilerParams(vmem_limit_bytes=2 * result_bytes + (2 << 20)),
    )(plan, coh)


def solution(mesh):
    placed = (P(("grp", "date"), None, "row", None), P())
    return jax.shard_map(
        functools.partial(body, mesh.shape["date"], mesh.shape["row"]),
        mesh=mesh,
        in_specs=placed,
        out_specs=P(("grp", "date"), None, None, "row", None),
        check_vma=False,
    )
```

```python
import functools

import jax
import jax.numpy as jnp
from jax import lax
from jax.experimental import pallas as pl
from jax.experimental.pallas import tpu as pltpu
from jax.sharding import PartitionSpec as P

HALF_ROWS = 4
HALF_COLS = 16
LANES = 128

epsilon = 1e-06


def gather_kernel(n, rows_n, x_ref, coh, own, edge, mid, top, bot, mine, other, band, pbuf, sbuf, lhs, pw,
                  load_sem, recv, right_send, left_send, top_recv, bot_recv, down_send, up_send):
    local, _, height, width = x_ref.shape
    tiles = width // LANES
    inner = height - 2 * HALF_ROWS
    span = height + 2 * HALF_ROWS
    me = lax.axis_index("date")
    row = lax.axis_index("row")
    has_left, has_right = me > 0, me < n - 1
    at_end = jnp.logical_not(jnp.logical_and(has_left, has_right))
    has_up, has_down = row > 0, row < rows_n - 1

    load = pltpu.make_async_copy(x_ref, own, load_sem)
    load.start()
    barrier = pltpu.get_barrier_semaphore()

    def greet(axis, index):
        pl.semaphore_signal(barrier, inc=1, device_id={axis: index}, device_id_type=pl.DeviceIdType.MESH)

    pl.when(has_left)(lambda: greet("date", me - 1))
    pl.when(has_right)(lambda: greet("date", me + 1))
    pl.when(has_up)(lambda: greet("row", row - 1))
    pl.when(has_down)(lambda: greet("row", row + 1))

    col_in = lax.broadcasted_iota(jnp.int32, (width, width), 0)
    col_out = lax.broadcasted_iota(jnp.int32, (width, width), 1)
    band[...] = jnp.where(jnp.abs(col_in - col_out) <= HALF_COLS, 1.0, 0.0).astype(jnp.bfloat16)

    @pl.when(row == 0)
    def _():
        top[...] = jnp.zeros_like(top)

    @pl.when(row == rows_n - 1)
    def _():
        bot[...] = jnp.zeros_like(bot)

    def remote(src, dst, send_sem, recv_sem, axis, index):
        return pltpu.make_async_remote_copy(
            src_ref=src, dst_ref=dst, send_sem=send_sem, recv_sem=recv_sem,
            device_id={axis: index}, device_id_type=pl.DeviceIdType.MESH)

    chunks = [(0, l) for l in range(local)] + [(1, l) for l in range(local)]

    def to_date(sends, step, k, s, l):
        ref = (edge, mid)[k].at[s, l]
        return remote(ref, ref, sends.at[k, s, l], recv.at[k, s, l], "date", me + step)

    def to_right(k, s, l):
        return to_date(right_send, 1, k, s, l)

    def to_left(k, s, l):
        return to_date(left_send, -1, k, s, l)

    def to_down(s, l):
        return remote(edge.at[s, l, 1], top.at[s, l], down_send.at[s, l], top_recv.at[s, l], "row", row + 1)

    def to_up(s, l):
        return remote(edge.at[s, l, 0], bot.at[s, l], up_send.at[s, l], bot_recv.at[s, l], "row", row - 1)

    def send_rims(s, l):
        pl.when(has_down)(lambda: to_down(s, l).start())
        pl.when(has_up)(lambda: to_up(s, l).start())

    def wait_rims(s, l):
        pl.when(has_up)(lambda: to_down(s, l).wait_recv())
        pl.when(has_down)(lambda: to_up(s, l).wait_recv())

    def wait_rims_sent(s, l):
        pl.when(has_down)(lambda: to_down(s, l).wait_send())
        pl.when(has_up)(lambda: to_up(s, l).wait_send())

    def assemble(dst, s, l):
        low = height + HALF_ROWS
        for part in range(2):
            for c in range(tiles):
                lanes = slice(c * LANES, (c + 1) * LANES)
                dst[part, c, 0:HALF_ROWS] = top[s, l, part, :, lanes]
                dst[part, c, HALF_ROWS:2 * HALF_ROWS] = edge[s, l, 0, part, :, lanes]
                dst[part, c, 2 * HALF_ROWS:2 * HALF_ROWS + inner] = mid[s, l, part, :, lanes]
                dst[part, c, height:low] = edge[s, l, 1, part, :, lanes]
                dst[part, c, low:low + HALF_ROWS] = bot[s, l, part, :, lanes]

    def window(fields):
        count = len(fields)
        for f, field in enumerate(fields):
            pbuf[f] = field
        for f in range(count):
            sbuf[f, :, 0:span - 2] = (pbuf[f, :, 0:span - 2] + pbuf[f, :, 1:span - 1]) + pbuf[f, :, 2:span]
        for f in range(count):
            total = (sbuf[f, :, 0:height] + sbuf[f, :, 3:height + 3]) + sbuf[f, :, 6:height + 6]
            high = total.astype(jnp.bfloat16)
            low = (total - high.astype(jnp.float32)).astype(jnp.bfloat16)
            for c in range(tiles):
                lhs[f * height:(f + 1) * height, c * LANES:(c + 1) * LANES] = high[c]
                lhs[(count + f) * height:(count + f + 1) * height, c * LANES:(c + 1) * LANES] = low[c]
        sums = jnp.dot(lhs[0:2 * count * height], band[...], preferred_element_type=jnp.float32)
        return [sums[f * height:(f + 1) * height] + sums[(count + f) * height:(count + f + 1) * height]
                for f in range(count)]

    def local_power():
        fields = []
        for i in range(local):
            real, imag = mine[i, 0], mine[i, 1]
            fields.append(real * real + imag * imag)
        for i, power in enumerate(window(fields)):
            pw[i] = power

    def compute(s, l, oth_real, oth_imag):
        fields = [oth_real * oth_real + oth_imag * oth_imag]
        for i in range(local):
            real, imag = mine[i, 0], mine[i, 1]
            fields.append(real * oth_real + imag * oth_imag)
            fields.append(imag * oth_real - real * oth_imag)
        sums = window(fields)
        date = s * local + l
        for i in range(local):
            factor = lax.rsqrt(pw[i] * sums[0] + epsilon)
            coh[i, date, 0] = sums[1 + 2 * i] * factor
            coh[i, date, 1] = sums[2 + 2 * i] * factor

    load.wait()
    for l in range(local):
        edge[me, l, 0] = own[l, :, 0:HALF_ROWS]
        edge[me, l, 1] = own[l, :, height - HALF_ROWS:height]
        mid[me, l] = own[l, :, HALF_ROWS:height - HALF_ROWS]
    greeters = functools.reduce(jnp.add, [jnp.where(near, 1, 0) for near in (has_left, has_right, has_up, has_down)])
    pl.semaphore_wait(barrier, greeters)

    for k, l in chunks:
        pl.when(has_right)(lambda: to_right(k, me, l).start())
        pl.when(has_left)(lambda: to_left(k, me, l).start())
        if k == 0:
            send_rims(me, l)
    def own_dates():
        for l in range(local):
            wait_rims(me, l)
            assemble(mine.at[l], me, l)
        local_power()
        for l in range(local):
            compute(me, l, mine[l, 0], mine[l, 1])

    def finish(t, l):
        for s, there in ((me - 1 - t, me - 1 - t >= 0), (me + 1 + t, me + 1 + t < n)):
            @pl.when(there)
            def _(s=s):
                wait_rims(s, l)
                assemble(other, s, l)
                compute(s, l, other[0], other[1])

    def step(t, carry):
        s_left, s_right = me - 1 - t, me + 1 + t
        for k, l in chunks:
            @pl.when(s_left >= 0)
            def _():
                to_right(k, s_left, l).wait_recv()
                pl.when(has_right)(lambda: to_right(k, s_left, l).start())
                if k == 0:
                    send_rims(s_left, l)

            @pl.when(s_right < n)
            def _():
                to_left(k, s_right, l).wait_recv()
                pl.when(has_left)(lambda: to_left(k, s_right, l).start())
                if k == 0:
                    send_rims(s_right, l)

            if k == 0 and l == local - 1:
                pl.when(jnp.logical_and(at_end, t == 0))(own_dates)
            if k == 1:
                pl.when(at_end)(lambda: finish(t, l))
        return carry

    if n > 1:
        lax.fori_loop(0, n - 1, step, 0)

        @pl.when(jnp.logical_not(at_end))
        def _():
            own_dates()

            def late(t, carry):
                for l in range(local):
                    finish(t, l)
                return carry

            lax.fori_loop(0, n - 1, late, 0)
    else:
        own_dates()

    for k, l in chunks:
        pl.when(has_right)(lambda: to_right(k, me, l).wait_send())
        pl.when(has_left)(lambda: to_left(k, me, l).wait_send())
        if k == 0:
            wait_rims_sent(me, l)

    def drain(t, carry):
        s_left, s_right = me - 1 - t, me + 1 + t
        for k, l in chunks:
            @pl.when(s_left >= 0)
            def _():
                pl.when(has_right)(lambda: to_right(k, s_left, l).wait_send())
                if k == 0:
                    wait_rims_sent(s_left, l)

            @pl.when(s_right < n)
            def _():
                pl.when(has_left)(lambda: to_left(k, s_right, l).wait_send())
                if k == 0:
                    wait_rims_sent(s_right, l)
        return carry

    if n > 1:
        lax.fori_loop(0, n - 1, drain, 0)


def order_kernel(plan_ref, coh, out, sem):
    dates = out.shape[1]

    def copy(k):
        return pltpu.make_async_copy(coh.at[:, plan_ref[k]], out.at[:, k], sem.at[k])

    def start(k, carry):
        copy(k).start()
        return carry

    def finish(k, carry):
        copy(k).wait()
        return carry

    lax.fori_loop(0, dates, start, 0)
    lax.fori_loop(0, dates, finish, 0)


def body(n, rows_n, stack_data, plan):
    local, _, height, width = stack_data.shape
    dates = local * n
    tiles = width // LANES
    fields = 2 * local + 1
    span = height + 2 * HALF_ROWS
    kind = jax.ShapeDtypeStruct((local, dates, 2, height, width), jnp.float32)
    dma = pltpu.SemaphoreType.DMA
    result_bytes = local * dates * 2 * height * width * 4
    stack_data = pltpu.with_memory_space_constraint(stack_data, pltpu.HBM)
    coh = pl.pallas_call(
        functools.partial(gather_kernel, n, rows_n),
        out_shape=kind,
        in_specs=[pl.BlockSpec(memory_space=pltpu.HBM)],
        out_specs=pl.BlockSpec(memory_space=pltpu.VMEM),
        scratch_shapes=[
            pltpu.VMEM((local, 2, height, width), jnp.float32),
            pltpu.VMEM((n, local, 2, 2, HALF_ROWS, width), jnp.float32),
            pltpu.VMEM((n, local, 2, height - 2 * HALF_ROWS, width), jnp.float32),
            pltpu.VMEM((n, local, 2, HALF_ROWS, width), jnp.float32),
            pltpu.VMEM((n, local, 2, HALF_ROWS, width), jnp.float32),
            pltpu.VMEM((local, 2, tiles, span, LANES), jnp.float32),
            pltpu.VMEM((2, tiles, span, LANES), jnp.float32),
            pltpu.VMEM((width, width), jnp.bfloat16),
            pltpu.VMEM((fields, tiles, span, LANES), jnp.float32),
            pltpu.VMEM((fields, tiles, span, LANES), jnp.float32),
            pltpu.VMEM((2 * fields * height, width), jnp.bfloat16),
            pltpu.VMEM((local, height, width), jnp.float32),
            dma,
            dma((2, n, local)), dma((2, n, local)), dma((2, n, local)),
            dma((n, local)), dma((n, local)), dma((n, local)), dma((n, local)),
        ],
        compiler_params=pltpu.CompilerParams(
            collective_id=0, has_side_effects=True,
            vmem_limit_bytes=4 * result_bytes + (8 << 20)),
    )(stack_data)
    return pl.pallas_call(
        order_kernel,
        out_shape=kind,
        in_specs=[pl.BlockSpec(memory_space=pltpu.SMEM), pl.BlockSpec(memory_space=pltpu.VMEM)],
        out_specs=pl.BlockSpec(memory_space=pl.ANY),
        scratch_shapes=[dma((dates,))],
        compiler_params=pltpu.CompilerParams(vmem_limit_bytes=2 * result_bytes + (2 << 20)),
    )(plan, coh)


def solution(mesh):
    placed = (P(("grp", "date"), None, "row", None), P())
    return jax.shard_map(
        functools.partial(body, mesh.shape["date"], mesh.shape["row"]),
        mesh=mesh,
        in_specs=placed,
        out_specs=P(("grp", "date"), None, None, "row", None),
        check_vma=False,
    )
```

```python
import functools

import jax
import jax.numpy as jnp
from jax import lax
from jax.experimental import pallas as pl
from jax.experimental.pallas import tpu as pltpu
from jax.sharding import PartitionSpec as P

HALF_ROWS = 4
HALF_COLS = 16
LANES = 128

epsilon = 1e-06


def gather_kernel(n, rows_n, x_ref, coh, own, edge, mid, top, bot, mine, other, band, pbuf, sbuf, lhs, pw,
                  load_sem, recv, right_send, left_send, top_recv, bot_recv, down_send, up_send):
    local, _, height, width = x_ref.shape
    tiles = width // LANES
    inner = height - 2 * HALF_ROWS
    span = height + 2 * HALF_ROWS
    me = lax.axis_index("date")
    row = lax.axis_index("row")
    has_left, has_right = me > 0, me < n - 1
    at_end = jnp.logical_not(jnp.logical_and(has_left, has_right))
    has_up, has_down = row > 0, row < rows_n - 1

    load = pltpu.make_async_copy(x_ref, own, load_sem)
    load.start()
    barrier = pltpu.get_barrier_semaphore()

    def greet(axis, index):
        pl.semaphore_signal(barrier, inc=1, device_id={axis: index}, device_id_type=pl.DeviceIdType.MESH)

    pl.when(has_left)(lambda: greet("date", me - 1))
    pl.when(has_right)(lambda: greet("date", me + 1))
    pl.when(has_up)(lambda: greet("row", row - 1))
    pl.when(has_down)(lambda: greet("row", row + 1))

    def remote(src, dst, send_sem, recv_sem, axis, index):
        return pltpu.make_async_remote_copy(
            src_ref=src, dst_ref=dst, send_sem=send_sem, recv_sem=recv_sem,
            device_id={axis: index}, device_id_type=pl.DeviceIdType.MESH)

    chunks = [(0, l) for l in range(local)] + [(1, l) for l in range(local)]

    def to_date(sends, step, k, s, l):
        ref = (edge, mid)[k].at[s, l]
        return remote(ref, ref, sends.at[k, s, l], recv.at[k, s, l], "date", me + step)

    def to_right(k, s, l):
        return to_date(right_send, 1, k, s, l)

    def to_left(k, s, l):
        return to_date(left_send, -1, k, s, l)

    def to_down(s, l):
        return remote(edge.at[s, l, 1], top.at[s, l], down_send.at[s, l], top_recv.at[s, l], "row", row + 1)

    def to_up(s, l):
        return remote(edge.at[s, l, 0], bot.at[s, l], up_send.at[s, l], bot_recv.at[s, l], "row", row - 1)

    def send_rims(s, l):
        pl.when(has_down)(lambda: to_down(s, l).start())
        pl.when(has_up)(lambda: to_up(s, l).start())

    def wait_rims(s, l):
        pl.when(has_up)(lambda: to_down(s, l).wait_recv())
        pl.when(has_down)(lambda: to_up(s, l).wait_recv())

    def wait_rims_sent(s, l):
        pl.when(has_down)(lambda: to_down(s, l).wait_send())
        pl.when(has_up)(lambda: to_up(s, l).wait_send())

    def assemble(dst, s, l):
        low = height + HALF_ROWS
        for part in range(2):
            for c in range(tiles):
                lanes = slice(c * LANES, (c + 1) * LANES)
                dst[part, c, 0:HALF_ROWS] = top[s, l, part, :, lanes]
                dst[part, c, HALF_ROWS:2 * HALF_ROWS] = edge[s, l, 0, part, :, lanes]
                dst[part, c, 2 * HALF_ROWS:2 * HALF_ROWS + inner] = mid[s, l, part, :, lanes]
                dst[part, c, height:low] = edge[s, l, 1, part, :, lanes]
                dst[part, c, low:low + HALF_ROWS] = bot[s, l, part, :, lanes]

    def window(fields):
        count = len(fields)
        for f, field in enumerate(fields):
            pbuf[f] = field
        for f in range(count):
            sbuf[f, :, 0:span - 2] = (pbuf[f, :, 0:span - 2] + pbuf[f, :, 1:span - 1]) + pbuf[f, :, 2:span]
        for f in range(count):
            total = (sbuf[f, :, 0:height] + sbuf[f, :, 3:height + 3]) + sbuf[f, :, 6:height + 6]
            high = total.astype(jnp.bfloat16)
            low = (total - high.astype(jnp.float32)).astype(jnp.bfloat16)
            for c in range(tiles):
                lhs[f * height:(f + 1) * height, c * LANES:(c + 1) * LANES] = high[c]
                lhs[(count + f) * height:(count + f + 1) * height, c * LANES:(c + 1) * LANES] = low[c]
        sums = jnp.dot(lhs[0:2 * count * height], band[...], preferred_element_type=jnp.float32)
        return [sums[f * height:(f + 1) * height] + sums[(count + f) * height:(count + f + 1) * height]
                for f in range(count)]

    def local_power():
        fields = []
        for i in range(local):
            real, imag = mine[i, 0], mine[i, 1]
            fields.append(real * real + imag * imag)
        for i, power in enumerate(window(fields)):
            pw[i] = power

    def compute(s, l, oth_real, oth_imag):
        fields = [oth_real * oth_real + oth_imag * oth_imag]
        for i in range(local):
            real, imag = mine[i, 0], mine[i, 1]
            fields.append(real * oth_real + imag * oth_imag)
            fields.append(imag * oth_real - real * oth_imag)
        sums = window(fields)
        date = s * local + l
        for i in range(local):
            factor = lax.rsqrt(pw[i] * sums[0] + epsilon)
            coh[i, date, 0] = sums[1 + 2 * i] * factor
            coh[i, date, 1] = sums[2 + 2 * i] * factor

    load.wait()
    for l in range(local):
        edge[me, l, 0] = own[l, :, 0:HALF_ROWS]
        edge[me, l, 1] = own[l, :, height - HALF_ROWS:height]
        mid[me, l] = own[l, :, HALF_ROWS:height - HALF_ROWS]
    greeters = functools.reduce(jnp.add, [jnp.where(near, 1, 0) for near in (has_left, has_right, has_up, has_down)])
    pl.semaphore_wait(barrier, greeters)

    for k, l in chunks:
        pl.when(has_left)(lambda: to_left(k, me, l).start())
        pl.when(has_right)(lambda: to_right(k, me, l).start())
        if k == 0:
            send_rims(me, l)
    col_in = lax.broadcasted_iota(jnp.int32, (width, width), 0)
    col_out = lax.broadcasted_iota(jnp.int32, (width, width), 1)
    band[...] = jnp.where(jnp.abs(col_in - col_out) <= HALF_COLS, 1.0, 0.0).astype(jnp.bfloat16)

    @pl.when(row == 0)
    def _():
        top[...] = jnp.zeros_like(top)

    @pl.when(row == rows_n - 1)
    def _():
        bot[...] = jnp.zeros_like(bot)

    def own_dates():
        for l in range(local):
            wait_rims(me, l)
            assemble(mine.at[l], me, l)
        local_power()
        for l in range(local):
            compute(me, l, mine[l, 0], mine[l, 1])

    def finish(t, l):
        for s, there in ((me - 1 - t, me - 1 - t >= 0), (me + 1 + t, me + 1 + t < n)):
            @pl.when(there)
            def _(s=s):
                wait_rims(s, l)
                assemble(other, s, l)
                compute(s, l, other[0], other[1])

    def step(t, carry):
        s_left, s_right = me - 1 - t, me + 1 + t
        for k, l in chunks:
            @pl.when(s_right < n)
            def _():
                to_left(k, s_right, l).wait_recv()
                pl.when(has_left)(lambda: to_left(k, s_right, l).start())
                if k == 0:
                    send_rims(s_right, l)

            @pl.when(s_left >= 0)
            def _():
                to_right(k, s_left, l).wait_recv()
                pl.when(has_right)(lambda: to_right(k, s_left, l).start())
                if k == 0:
                    send_rims(s_left, l)

            if k == 0 and l == local - 1:
                pl.when(jnp.logical_and(at_end, t == 0))(own_dates)
            if k == 1:
                pl.when(at_end)(lambda: finish(t, l))
        return carry

    if n > 1:
        lax.fori_loop(0, n - 1, step, 0)

        @pl.when(jnp.logical_not(at_end))
        def _():
            own_dates()

            def late(t, carry):
                for l in range(local):
                    finish(t, l)
                return carry

            lax.fori_loop(0, n - 1, late, 0)
    else:
        own_dates()

    for k, l in chunks:
        pl.when(has_right)(lambda: to_right(k, me, l).wait_send())
        pl.when(has_left)(lambda: to_left(k, me, l).wait_send())
        if k == 0:
            wait_rims_sent(me, l)

    def drain(t, carry):
        s_left, s_right = me - 1 - t, me + 1 + t
        for k, l in chunks:
            @pl.when(s_left >= 0)
            def _():
                pl.when(has_right)(lambda: to_right(k, s_left, l).wait_send())
                if k == 0:
                    wait_rims_sent(s_left, l)

            @pl.when(s_right < n)
            def _():
                pl.when(has_left)(lambda: to_left(k, s_right, l).wait_send())
                if k == 0:
                    wait_rims_sent(s_right, l)
        return carry

    if n > 1:
        lax.fori_loop(0, n - 1, drain, 0)


def order_kernel(plan_ref, coh, out, sem):
    dates = out.shape[1]

    def copy(k):
        return pltpu.make_async_copy(coh.at[:, plan_ref[k]], out.at[:, k], sem.at[k])

    def start(k, carry):
        copy(k).start()
        return carry

    def finish(k, carry):
        copy(k).wait()
        return carry

    lax.fori_loop(0, dates, start, 0)
    lax.fori_loop(0, dates, finish, 0)


def body(n, rows_n, stack_data, plan):
    local, _, height, width = stack_data.shape
    dates = local * n
    tiles = width // LANES
    fields = 2 * local + 1
    span = height + 2 * HALF_ROWS
    kind = jax.ShapeDtypeStruct((local, dates, 2, height, width), jnp.float32)
    dma = pltpu.SemaphoreType.DMA
    result_bytes = local * dates * 2 * height * width * 4
    stack_data = pltpu.with_memory_space_constraint(stack_data, pltpu.HBM)
    coh = pl.pallas_call(
        functools.partial(gather_kernel, n, rows_n),
        out_shape=kind,
        in_specs=[pl.BlockSpec(memory_space=pltpu.HBM)],
        out_specs=pl.BlockSpec(memory_space=pltpu.VMEM),
        scratch_shapes=[
            pltpu.VMEM((local, 2, height, width), jnp.float32),
            pltpu.VMEM((n, local, 2, 2, HALF_ROWS, width), jnp.float32),
            pltpu.VMEM((n, local, 2, height - 2 * HALF_ROWS, width), jnp.float32),
            pltpu.VMEM((n, local, 2, HALF_ROWS, width), jnp.float32),
            pltpu.VMEM((n, local, 2, HALF_ROWS, width), jnp.float32),
            pltpu.VMEM((local, 2, tiles, span, LANES), jnp.float32),
            pltpu.VMEM((2, tiles, span, LANES), jnp.float32),
            pltpu.VMEM((width, width), jnp.bfloat16),
            pltpu.VMEM((fields, tiles, span, LANES), jnp.float32),
            pltpu.VMEM((fields, tiles, span, LANES), jnp.float32),
            pltpu.VMEM((2 * fields * height, width), jnp.bfloat16),
            pltpu.VMEM((local, height, width), jnp.float32),
            dma,
            dma((2, n, local)), dma((2, n, local)), dma((2, n, local)),
            dma((n, local)), dma((n, local)), dma((n, local)), dma((n, local)),
        ],
        compiler_params=pltpu.CompilerParams(
            collective_id=0, has_side_effects=True,
            vmem_limit_bytes=4 * result_bytes + (8 << 20)),
    )(stack_data)
    return pl.pallas_call(
        order_kernel,
        out_shape=kind,
        in_specs=[pl.BlockSpec(memory_space=pltpu.SMEM), pl.BlockSpec(memory_space=pltpu.VMEM)],
        out_specs=pl.BlockSpec(memory_space=pl.ANY),
        scratch_shapes=[dma((dates,))],
        compiler_params=pltpu.CompilerParams(vmem_limit_bytes=2 * result_bytes + (2 << 20)),
    )(plan, coh)


def solution(mesh):
    placed = (P(("grp", "date"), None, "row", None), P())
    return jax.shard_map(
        functools.partial(body, mesh.shape["date"], mesh.shape["row"]),
        mesh=mesh,
        in_specs=placed,
        out_specs=P(("grp", "date"), None, None, "row", None),
        check_vma=False,
    )
```

```python
import functools

import jax
import jax.numpy as jnp
from jax import lax
from jax.experimental import pallas as pl
from jax.experimental.pallas import tpu as pltpu
from jax.sharding import PartitionSpec as P

HALF_ROWS = 4
HALF_COLS = 16
LANES = 128

epsilon = 1e-06


def gather_kernel(n, rows_n, x_ref, coh, own, edge, mid, top, bot, mine, other, band, pbuf, sbuf, lhs, pw,
                  load_sem, recv, right_send, left_send, top_recv, bot_recv, down_send, up_send):
    local, _, height, width = x_ref.shape
    tiles = width // LANES
    inner = height - 2 * HALF_ROWS
    span = height + 2 * HALF_ROWS
    me = lax.axis_index("date")
    row = lax.axis_index("row")
    has_left, has_right = me > 0, me < n - 1
    at_end = jnp.logical_not(jnp.logical_and(has_left, has_right))
    has_up, has_down = row > 0, row < rows_n - 1

    load = pltpu.make_async_copy(x_ref, own, load_sem)
    load.start()
    barrier = pltpu.get_barrier_semaphore()

    def greet(axis, index):
        pl.semaphore_signal(barrier, inc=1, device_id={axis: index}, device_id_type=pl.DeviceIdType.MESH)

    pl.when(has_left)(lambda: greet("date", me - 1))
    pl.when(has_right)(lambda: greet("date", me + 1))
    pl.when(has_up)(lambda: greet("row", row - 1))
    pl.when(has_down)(lambda: greet("row", row + 1))

    def remote(src, dst, send_sem, recv_sem, axis, index):
        return pltpu.make_async_remote_copy(
            src_ref=src, dst_ref=dst, send_sem=send_sem, recv_sem=recv_sem,
            device_id={axis: index}, device_id_type=pl.DeviceIdType.MESH)

    chunks = [(0, l) for l in range(local)] + [(1, l) for l in range(local)]

    def to_date(sends, step, k, s, l):
        ref = (edge, mid)[k].at[s, l]
        return remote(ref, ref, sends.at[k, s, l], recv.at[k, s, l], "date", me + step)

    def to_right(k, s, l):
        return to_date(right_send, 1, k, s, l)

    def to_left(k, s, l):
        return to_date(left_send, -1, k, s, l)

    def to_down(s, l):
        return remote(edge.at[s, l, 1], top.at[s, l], down_send.at[s, l], top_recv.at[s, l], "row", row + 1)

    def to_up(s, l):
        return remote(edge.at[s, l, 0], bot.at[s, l], up_send.at[s, l], bot_recv.at[s, l], "row", row - 1)

    def send_rims(s, l):
        pl.when(has_down)(lambda: to_down(s, l).start())
        pl.when(has_up)(lambda: to_up(s, l).start())

    def wait_rims(s, l):
        pl.when(has_up)(lambda: to_down(s, l).wait_recv())
        pl.when(has_down)(lambda: to_up(s, l).wait_recv())

    def wait_rims_sent(s, l):
        pl.when(has_down)(lambda: to_down(s, l).wait_send())
        pl.when(has_up)(lambda: to_up(s, l).wait_send())

    def assemble(dst, s, l):
        low = height + HALF_ROWS
        for part in range(2):
            for c in range(tiles):
                lanes = slice(c * LANES, (c + 1) * LANES)
                dst[part, c, 0:HALF_ROWS] = top[s, l, part, :, lanes]
                dst[part, c, HALF_ROWS:2 * HALF_ROWS] = edge[s, l, 0, part, :, lanes]
                dst[part, c, 2 * HALF_ROWS:2 * HALF_ROWS + inner] = mid[s, l, part, :, lanes]
                dst[part, c, height:low] = edge[s, l, 1, part, :, lanes]
                dst[part, c, low:low + HALF_ROWS] = bot[s, l, part, :, lanes]

    def window(fields):
        count = len(fields)
        for f, field in enumerate(fields):
            pbuf[f] = field
        for f in range(count):
            sbuf[f, :, 0:span - 2] = (pbuf[f, :, 0:span - 2] + pbuf[f, :, 1:span - 1]) + pbuf[f, :, 2:span]
        for f in range(count):
            total = (sbuf[f, :, 0:height] + sbuf[f, :, 3:height + 3]) + sbuf[f, :, 6:height + 6]
            high = total.astype(jnp.bfloat16)
            low = (total - high.astype(jnp.float32)).astype(jnp.bfloat16)
            for c in range(tiles):
                lhs[f * height:(f + 1) * height, c * LANES:(c + 1) * LANES] = high[c]
                lhs[(count + f) * height:(count + f + 1) * height, c * LANES:(c + 1) * LANES] = low[c]
        sums = jnp.dot(lhs[0:2 * count * height], band[...], preferred_element_type=jnp.float32)
        return [sums[f * height:(f + 1) * height] + sums[(count + f) * height:(count + f + 1) * height]
                for f in range(count)]

    def local_power():
        fields = []
        for i in range(local):
            real, imag = mine[i, 0], mine[i, 1]
            fields.append(real * real + imag * imag)
        for i, power in enumerate(window(fields)):
            pw[i] = power

    def compute(s, l, oth_real, oth_imag):
        fields = [oth_real * oth_real + oth_imag * oth_imag]
        for i in range(local):
            real, imag = mine[i, 0], mine[i, 1]
            fields.append(real * oth_real + imag * oth_imag)
            fields.append(imag * oth_real - real * oth_imag)
        sums = window(fields)
        date = s * local + l
        for i in range(local):
            factor = lax.rsqrt(pw[i] * sums[0] + epsilon)
            coh[i, date, 0] = sums[1 + 2 * i] * factor
            coh[i, date, 1] = sums[2 + 2 * i] * factor

    load.wait()
    for l in range(local):
        edge[me, l, 0] = own[l, :, 0:HALF_ROWS]
        edge[me, l, 1] = own[l, :, height - HALF_ROWS:height]
        mid[me, l] = own[l, :, HALF_ROWS:height - HALF_ROWS]
    greeters = functools.reduce(jnp.add, [jnp.where(near, 1, 0) for near in (has_left, has_right, has_up, has_down)])
    pl.semaphore_wait(barrier, greeters)

    for k, l in chunks:
        pl.when(has_left)(lambda: to_left(k, me, l).start())
        pl.when(has_right)(lambda: to_right(k, me, l).start())
        if k == 0:
            send_rims(me, l)
    col_in = lax.broadcasted_iota(jnp.int32, (width, width), 0)
    col_out = lax.broadcasted_iota(jnp.int32, (width, width), 1)
    band[...] = jnp.where(jnp.abs(col_in - col_out) <= HALF_COLS, 1.0, 0.0).astype(jnp.bfloat16)

    @pl.when(row == 0)
    def _():
        top[...] = jnp.zeros_like(top)

    @pl.when(row == rows_n - 1)
    def _():
        bot[...] = jnp.zeros_like(bot)

    def own_dates():
        for l in range(local):
            wait_rims(me, l)
            assemble(mine.at[l], me, l)
        local_power()
        for l in range(local):
            compute(me, l, mine[l, 0], mine[l, 1])

    def finish(t, l):
        for s, there in ((me - 1 - t, me - 1 - t >= 0), (me + 1 + t, me + 1 + t < n)):
            @pl.when(there)
            def _(s=s):
                wait_rims(s, l)
                assemble(other, s, l)
                compute(s, l, other[0], other[1])

    def step(t, carry):
        s_left, s_right = me - 1 - t, me + 1 + t
        for k, l in chunks:
            @pl.when(s_right < n)
            def _():
                to_left(k, s_right, l).wait_recv()
                pl.when(has_left)(lambda: to_left(k, s_right, l).start())
                if k == 0:
                    send_rims(s_right, l)

            @pl.when(s_left >= 0)
            def _():
                to_right(k, s_left, l).wait_recv()
                pl.when(has_right)(lambda: to_right(k, s_left, l).start())
                if k == 0:
                    send_rims(s_left, l)

            if k == 0 and l == local - 1:
                pl.when(jnp.logical_and(at_end, t == 0))(own_dates)
            if k == 1:
                pl.when(at_end)(lambda: finish(t, l))
        return carry

    if n > 1:
        lax.fori_loop(0, n - 1, step, 0)

        @pl.when(jnp.logical_not(at_end))
        def _():
            own_dates()

            def late(t, carry):
                for l in range(local):
                    finish(t, l)
                return carry

            lax.fori_loop(0, n - 1, late, 0)
    else:
        own_dates()

    for k, l in chunks:
        pl.when(has_right)(lambda: to_right(k, me, l).wait_send())
        pl.when(has_left)(lambda: to_left(k, me, l).wait_send())
        if k == 0:
            wait_rims_sent(me, l)

    def drain(t, carry):
        s_left, s_right = me - 1 - t, me + 1 + t
        for k, l in chunks:
            @pl.when(s_left >= 0)
            def _():
                pl.when(has_right)(lambda: to_right(k, s_left, l).wait_send())
                if k == 0:
                    wait_rims_sent(s_left, l)

            @pl.when(s_right < n)
            def _():
                pl.when(has_left)(lambda: to_left(k, s_right, l).wait_send())
                if k == 0:
                    wait_rims_sent(s_right, l)
        return carry

    if n > 1:
        lax.fori_loop(0, n - 1, drain, 0)


def order_kernel(plan_ref, coh, out, sem):
    dates = out.shape[1]

    def copy(k):
        return pltpu.make_async_copy(coh.at[:, plan_ref[k]], out.at[:, k], sem.at[k])

    for k in range(dates):
        copy(k).start()
    for k in range(dates):
        copy(k).wait()


def body(n, rows_n, stack_data, plan):
    local, _, height, width = stack_data.shape
    dates = local * n
    tiles = width // LANES
    fields = 2 * local + 1
    span = height + 2 * HALF_ROWS
    kind = jax.ShapeDtypeStruct((local, dates, 2, height, width), jnp.float32)
    dma = pltpu.SemaphoreType.DMA
    result_bytes = local * dates * 2 * height * width * 4
    stack_data = pltpu.with_memory_space_constraint(stack_data, pltpu.HBM)
    coh = pl.pallas_call(
        functools.partial(gather_kernel, n, rows_n),
        out_shape=kind,
        in_specs=[pl.BlockSpec(memory_space=pltpu.HBM)],
        out_specs=pl.BlockSpec(memory_space=pltpu.VMEM),
        scratch_shapes=[
            pltpu.VMEM((local, 2, height, width), jnp.float32),
            pltpu.VMEM((n, local, 2, 2, HALF_ROWS, width), jnp.float32),
            pltpu.VMEM((n, local, 2, height - 2 * HALF_ROWS, width), jnp.float32),
            pltpu.VMEM((n, local, 2, HALF_ROWS, width), jnp.float32),
            pltpu.VMEM((n, local, 2, HALF_ROWS, width), jnp.float32),
            pltpu.VMEM((local, 2, tiles, span, LANES), jnp.float32),
            pltpu.VMEM((2, tiles, span, LANES), jnp.float32),
            pltpu.VMEM((width, width), jnp.bfloat16),
            pltpu.VMEM((fields, tiles, span, LANES), jnp.float32),
            pltpu.VMEM((fields, tiles, span, LANES), jnp.float32),
            pltpu.VMEM((2 * fields * height, width), jnp.bfloat16),
            pltpu.VMEM((local, height, width), jnp.float32),
            dma,
            dma((2, n, local)), dma((2, n, local)), dma((2, n, local)),
            dma((n, local)), dma((n, local)), dma((n, local)), dma((n, local)),
        ],
        compiler_params=pltpu.CompilerParams(
            collective_id=0, has_side_effects=True,
            vmem_limit_bytes=4 * result_bytes + (8 << 20)),
    )(stack_data)
    return pl.pallas_call(
        order_kernel,
        out_shape=kind,
        in_specs=[pl.BlockSpec(memory_space=pltpu.SMEM), pl.BlockSpec(memory_space=pltpu.VMEM)],
        out_specs=pl.BlockSpec(memory_space=pl.ANY),
        scratch_shapes=[dma((dates,))],
        compiler_params=pltpu.CompilerParams(vmem_limit_bytes=2 * result_bytes + (2 << 20)),
    )(plan, coh)


def solution(mesh):
    placed = (P(("grp", "date"), None, "row", None), P())
    return jax.shard_map(
        functools.partial(body, mesh.shape["date"], mesh.shape["row"]),
        mesh=mesh,
        in_specs=placed,
        out_specs=P(("grp", "date"), None, None, "row", None),
        check_vma=False,
    )
```
